512 devices in a mesh: section: 8 (over z_hi, x), ctx: 64 (over y, z_lo, core).
Axes of the slice: x: 4, y: 8, z: 8 (z_hi: 2, z_lo: 4; z = z_hi * 4 + z_lo), core: 2. Of those that a mesh axis runs over, the one named last changes fastest.
Arguments:
- resid: bfloat16 [8, 16384, 4096], P('section', 'ctx'), may hold values from -16 to 16
- queries: bfloat16 [8, 16384, 512], P('section', 'ctx'), may hold values from -8 to 8
- keyvals: bfloat16 [8, 16384, 256], P('section', 'ctx'), may hold values from -8 to 8
- run_max: float32 [8, 16384, 4], P('section', 'ctx'), may hold values from 1 to 4
- run_sum: float32 [8, 16384, 4], P('section', 'ctx'), may hold values from 128 to 1024
- run_out: float32 [8, 16384, 512], P('section', 'ctx'), may hold values from -384 to 384
- span_pair: int32 [64, 2], replicated, may hold values from 0 to 127, as said below
- norm_gain: float32 [8, 4096], P('section'), may hold values from 0.5 to 1.5
- w_query: bfloat16 [8, 4096, 512], P('section', 'ctx'), may hold values from -0.095458984 to 0.095458984
- w_keyval: bfloat16 [8, 4096, 256], P('section', 'ctx'), may hold values from -0.095458984 to 0.095458984
- w_out: bfloat16 [8, 512, 4096], P('section', None, 'ctx'), may hold values from -0.59765625 to 0.59765625
Outputs:
- queries_next: bfloat16 [8, 16384, 512], P('section', 'ctx')
- keyvals_next: bfloat16 [8, 16384, 256], P('section', 'ctx')
- max_next: float32 [8, 16384, 4], P('section', 'ctx')
- sum_next: float32 [8, 16384, 4], P('section', 'ctx')
- out_next: float32 [8, 16384, 512], P('section', 'ctx')
The draws below stay inside these ranges and needn't reach their ends.
Inputs may be any that keep to these rules, and one draw needn't show every extreme that they name: `span_pair`: each ctx index holds blocks c and 127 - c, its first column running once over 0 to 63.
All inputs are finite; a program needn't handle non-finite values.
Results may differ from the reference program's by a relative error of at most 0.005.
The reference program's roundings to bfloat16 on the way (of `attended`, `finished`, `incoming` and `normed`) count: a program that leaves them out, or rounds other values in their place, can miss the bound.
Values may be sent and summed in bfloat16 or wider, within the bound.
No kernel may reach another device: no remote copies, remote signals or barrier semaphores. Data moves between devices by JAX's collectives and lax.ppermute only.
A program may use at most 64 MiB of HBM per device.

```python
import math
import jax
import jax.numpy as jnp
from jax import lax

D = 4096
HEAD = 128
QHEADS = 4
TOK_DEV = 256
SPAN = 128
SEQ = 16384
SECTIONS = 8


def sign_vector(key, length):
    bits = jax.random.randint(key, (length,), 0, 2)
    return jnp.where(bits == 0, -1.0, 1.0).astype(jnp.float32)


def base_noise(key, shape):
    values = jnp.clip(jax.random.normal(key, shape, jnp.float32), -6.0, 6.0)
    return values


def row_levels(key, shape, lower, upper):
    chosen = jax.random.randint(jax.random.fold_in(key, 1), shape, 0, 16) == 0
    strength = jax.random.uniform(jax.random.fold_in(key, 2), shape, jnp.float32, lower, upper)
    return jnp.where(chosen, strength, 0.0).astype(jnp.float32)


def draw_span_pair(key, part):
    cycle_size = SEQ // TOK_DEV
    shuffled = jax.random.permutation(key, cycle_size).astype(jnp.int32)
    return jnp.stack([shuffled, 2 * cycle_size - 1 - shuffled], axis=-1).astype(jnp.int32)


def draw_resid(key, part):
    sigma = sign_vector(jax.random.fold_in(key, 11), D)

    def one_section(section):
        local = jax.random.fold_in(jax.random.fold_in(key, 21), section)
        noise = base_noise(jax.random.fold_in(local, 3), (SEQ, D))
        level = row_levels(local, (SEQ, 1), 5.0, 8.0)
        return (noise + level * sigma[None, :]).astype(jnp.bfloat16)
    return lax.map(one_section, jnp.arange(SECTIONS, dtype=jnp.int32))


def draw_w_query(key, part):
    sigma = sign_vector(jax.random.fold_in(key, 11), D)
    tau = sign_vector(jax.random.fold_in(key, 12), HEAD)
    local = jax.random.fold_in(key, 31)
    noise = base_noise(jax.random.fold_in(local, 1), (SECTIONS, D, QHEADS, HEAD)) * D ** (-0.5)
    head_level = jax.random.uniform(jax.random.fold_in(local, 2), (SECTIONS, 1, QHEADS, 1), jnp.float32, 4.0, 6.5)
    aligned = head_level * sigma[None, :, None, None] * tau[None, None, None, :] * (1.0 / D)
    return (noise + aligned).reshape(SECTIONS, D, QHEADS * HEAD).astype(jnp.bfloat16)


def draw_w_keyval(key, part):
    sigma = sign_vector(jax.random.fold_in(key, 11), D)
    tau = sign_vector(jax.random.fold_in(key, 12), HEAD)
    local = jax.random.fold_in(key, 41)
    noise = base_noise(jax.random.fold_in(local, 1), (SECTIONS, D, 2 * HEAD)) * D ** (-0.5)
    key_level = jax.random.uniform(jax.random.fold_in(local, 2), (SECTIONS, 1, 1), jnp.float32, 4.5, 6.0)
    aligned = key_level * sigma[None, :, None] * tau[None, None, :] * (1.0 / D)
    aligned = jnp.concatenate([aligned, jnp.zeros((SECTIONS, D, HEAD), jnp.float32)], axis=-1)
    return (noise + aligned).astype(jnp.bfloat16)


def draw_queries(key, part):
    tau = sign_vector(jax.random.fold_in(key, 13), HEAD)
    local = jax.random.fold_in(key, 51)
    noise = base_noise(jax.random.fold_in(local, 3), (SECTIONS, SEQ, QHEADS, HEAD))
    level = row_levels(local, (SECTIONS, SEQ, 1, 1), 3.5, 6.0)
    values = jnp.where(level > 0.0, level * tau[None, None, None, :] + 0.3 * noise, noise)
    return values.reshape(SECTIONS, SEQ, QHEADS * HEAD).astype(jnp.bfloat16)


def draw_keyvals(key, part):
    tau = sign_vector(jax.random.fold_in(key, 13), HEAD)
    local = jax.random.fold_in(key, 61)
    key_noise = base_noise(jax.random.fold_in(local, 3), (SECTIONS, SEQ, HEAD))
    value_noise = base_noise(jax.random.fold_in(local, 4), (SECTIONS, SEQ, HEAD))
    level = row_levels(local, (SECTIONS, SEQ, 1), 4.0, 6.0)
    key_part = jnp.where(level > 0.0, level * tau[None, None, :] + 0.3 * key_noise, key_noise)
    return jnp.concatenate([key_part, value_noise], axis=-1).astype(jnp.bfloat16)


def shard_levels(key, shape, shards, low, high):
    loudness = 1.0
    for position, shards_of in shards:
        steps = jax.random.uniform(jax.random.fold_in(jax.random.fold_in(key, 6), position), (shards_of,), jnp.float32, low / len(shards), high / len(shards))
        loudness = loudness * jnp.repeat(jnp.exp(steps), shape[position] // shards_of).reshape((-1,) + (1,) * (len(shape) - 1 - position))
    return loudness


def gaussian(rng, shape, width, reach, pieces=(), kind=jnp.bfloat16):
    factor_of = shard_levels(rng, shape, pieces, -0.22, 0.18) if pieces else 1.0
    result = jax.random.normal(rng, shape, jnp.float32) * width * factor_of
    return jnp.minimum(jnp.maximum(result, -reach), reach).astype(kind)


def setup_inputs(seed: int = 0) -> dict:
    streams_of = jax.random.split(jax.random.key(seed), 12)
    resid = draw_resid(jax.random.fold_in(streams_of[11], 71), 0)
    queries = draw_queries(jax.random.fold_in(streams_of[11], 71), 0)
    keyvals = draw_keyvals(jax.random.fold_in(streams_of[11], 71), 0)
    run_max = jnp.clip(1.0 + 3.0 * jax.random.uniform(streams_of[3], (SECTIONS, SEQ, QHEADS), jnp.float32) ** shard_levels(streams_of[3], (SECTIONS, SEQ, QHEADS), ((0, 8), (1, 64)), -0.2, 0.2), 1.0, 4.0)
    run_sum = jnp.clip(jnp.exp(math.log(1024.0) - 2.0794415 * jax.random.uniform(streams_of[4], (SECTIONS, SEQ, QHEADS), jnp.float32) ** shard_levels(streams_of[4], (SECTIONS, SEQ, QHEADS), ((0, 8), (1, 64)), -0.2, 0.2)), 128.0, 1024.0)
    run_out = gaussian(streams_of[5], (SECTIONS, SEQ, QHEADS * HEAD), (SPAN // 2), 384.0, ((0, 8), (1, 64)), jnp.float32)
    span_pair = draw_span_pair(jax.random.fold_in(streams_of[11], 71), 0)
    norm_gain = jnp.clip(1.0 + 0.1 * jax.random.normal(streams_of[7], (SECTIONS, D), jnp.float32), 0.5, 1.5)
    w_query = draw_w_query(jax.random.fold_in(streams_of[11], 71), 0)
    w_keyval = draw_w_keyval(jax.random.fold_in(streams_of[11], 71), 0)
    w_out = gaussian(streams_of[10], (SECTIONS, QHEADS * HEAD, D), 0.1, 0.59765625, ((0, 8), (2, 64)))
    return dict(resid=resid, queries=queries, keyvals=keyvals, run_max=run_max, run_sum=run_sum, run_out=run_out, span_pair=span_pair, norm_gain=norm_gain, w_query=w_query, w_keyval=w_keyval, w_out=w_out)


def positions(span_pair, rows_here):
    half_rows = rows_here // 2
    offsets = jnp.arange(rows_here, dtype=jnp.int32)
    span_index = span_pair[:, offsets // half_rows]
    return (span_index * half_rows + offsets % half_rows).astype(jnp.int32)

def flash_step(query_rows, key_block, pos_query, pos_key, old_max, old_sum, old_out):
    rows_here = query_rows.shape[0]
    query_heads = query_rows.reshape(rows_here, QHEADS, HEAD).astype(jnp.float32)
    key_part = key_block[:, :HEAD].astype(jnp.float32)
    value_part = key_block[:, HEAD:].astype(jnp.float32)
    scores = jnp.einsum('qhd,kd->hqk', query_heads, key_part) * HEAD ** (-0.5)
    keep = pos_key[None, None, :] <= pos_query[None, :, None]
    masked = jnp.where(keep, scores, -1e+30)
    prior_max = old_max.T
    new_max = jnp.maximum(prior_max, lax.optimization_barrier(jnp.max(masked, axis=-1)))
    exp_scores = jnp.where(keep, jnp.exp(scores - new_max[:, :, None]), 0.0)
    decay_factor = jnp.exp(prior_max - new_max)
    new_sum = old_sum.T * decay_factor + lax.optimization_barrier(jnp.sum(exp_scores, axis=-1))
    rounded = exp_scores.astype(jnp.bfloat16).astype(jnp.float32)
    contrib = jnp.einsum('hqk,kd->qhd', rounded, value_part)
    new_out = old_out.reshape(rows_here, QHEADS, HEAD) * decay_factor.T[:, :, None] + contrib
    return (new_max.T, new_sum.T, new_out.reshape(rows_here, QHEADS * HEAD))

def reference(resid, queries, keyvals, run_max, run_sum, run_out, span_pair, norm_gain, w_query, w_keyval, w_out):
    cycle_size = span_pair.shape[0]
    sections = resid.shape[0]
    rows_here = resid.shape[1] // cycle_size
    pos_all = positions(span_pair, rows_here)
    pos_near = jnp.roll(pos_all, -1, axis=0)
    pos_far = jnp.roll(pos_all, -2, axis=0)
    finished = []
    for section_index in range(sections):
        query_dev = queries[section_index].reshape(cycle_size, rows_here, -1)
        keyval_dev = keyvals[section_index].reshape(cycle_size, rows_here, -1)
        near_block = jnp.roll(keyval_dev, -1, axis=0)
        far_block = jnp.roll(keyval_dev, -2, axis=0)
        max_dev = run_max[section_index].reshape(cycle_size, rows_here, -1)
        sum_dev = run_sum[section_index].reshape(cycle_size, rows_here, -1)
        out_dev = run_out[section_index].reshape(cycle_size, rows_here, -1)

        def per_device(inputs_one):
            query_one, far_one, near_one, pos_q, pos_f, pos_n, max_one, sum_one, out_one = inputs_one
            max_one, sum_one, out_one = flash_step(query_one, far_one, pos_q, pos_f, max_one, sum_one, out_one)
            max_one, sum_one, out_one = flash_step(query_one, near_one, pos_q, pos_n, max_one, sum_one, out_one)
            divided = out_one.reshape(rows_here, QHEADS, HEAD) / sum_one[:, :, None]
            return divided.reshape(rows_here, QHEADS * HEAD).astype(jnp.bfloat16)
        attended = lax.map(per_device, (query_dev, far_block, near_block, pos_all, pos_far, pos_near, max_dev, sum_dev, out_dev))
        attended = attended.reshape(cycle_size * rows_here, -1)
        projected = jnp.dot(attended, w_out[section_index], preferred_element_type=jnp.float32)
        finished.append((resid[section_index].astype(jnp.float32) + projected).astype(jnp.bfloat16))
    outs_query, outs_keyval, outs_max, outs_sum, outs_out = ([], [], [], [], [])
    for section_index in range(sections):
        incoming = finished[(section_index - 1) % sections]
        wide = incoming.astype(jnp.float32)
        mean_square = lax.optimization_barrier(jnp.mean(wide * wide, axis=-1, keepdims=True))
        normed = (wide * lax.rsqrt(mean_square + 1e-05) * norm_gain[section_index][None, :]).astype(jnp.bfloat16)
        query_new = jnp.dot(normed, w_query[section_index], preferred_element_type=jnp.float32).astype(jnp.bfloat16)
        keyval_new = jnp.dot(normed, w_keyval[section_index], preferred_element_type=jnp.float32).astype(jnp.bfloat16)
        query_dev = query_new.reshape(cycle_size, rows_here, -1)
        keyval_dev = keyval_new.reshape(cycle_size, rows_here, -1)

        def first_step(inputs_one):
            query_one, keyval_one, pos_q = inputs_one
            start_max = jnp.full((rows_here, QHEADS), -1e+30, jnp.float32)
            start_sum = jnp.zeros((rows_here, QHEADS), jnp.float32)
            start_out = jnp.zeros((rows_here, QHEADS * HEAD), jnp.float32)
            return flash_step(query_one, keyval_one, pos_q, pos_q, start_max, start_sum, start_out)
        max_new, sum_new, out_new = lax.map(first_step, (query_dev, keyval_dev, pos_all))
        outs_query.append(query_new)
        outs_keyval.append(keyval_new)
        outs_max.append(max_new.reshape(cycle_size * rows_here, -1))
        outs_sum.append(sum_new.reshape(cycle_size * rows_here, -1))
        outs_out.append(out_new.reshape(cycle_size * rows_here, -1))
    return (jnp.stack(outs_query), jnp.stack(outs_keyval), jnp.stack(outs_max), jnp.stack(outs_sum), jnp.stack(outs_out))
```

```python
import functools

import jax
import jax.numpy as jnp
from jax import lax
from jax.experimental import pallas as pl
from jax.experimental.pallas import tpu as pltpu
from jax.sharding import Mesh
from jax.sharding import PartitionSpec as P

HEAD = 128
QHEADS = 4
SECT = ("zh", "x")
CTX = ("y", "zl", "c")
NY, NZ, NC, NS = 8, 4, 2, 8
SHARD = 64
BLOCK = NZ * NC * SHARD
NQ = QHEADS * HEAD
NKV = 2 * HEAD


def ring(count, steps):
    return [(source, (source + steps) % count) for source in range(count)]


def device_positions(span_pair, device, rows_here):
    half_rows = rows_here // 2
    span_row = lax.dynamic_slice_in_dim(span_pair, device, 1, 0)[0]
    offsets = jnp.arange(rows_here, dtype=jnp.int32)
    span_index = jnp.where(offsets < half_rows, span_row[0], span_row[1])
    return span_index * half_rows + offsets % half_rows


def flash_step(query_rows, key_block, pos_query, pos_key, old_max, old_sum, old_out):
    rows_here = query_rows.shape[0]
    query_heads = query_rows.reshape(rows_here, QHEADS, HEAD)
    key_part = key_block[:, :HEAD]
    value_part = key_block[:, HEAD:]
    scores = jnp.einsum(
        "qhd,kd->hqk", query_heads, key_part, preferred_element_type=jnp.float32
    ) * HEAD ** (-0.5)
    keep = pos_key[None, None, :] <= pos_query[None, :, None]
    masked = jnp.where(keep, scores, -1e30)
    prior_max = old_max.T
    new_max = jnp.maximum(prior_max, jnp.max(masked, axis=-1))
    exp_scores = jnp.where(keep, jnp.exp(scores - new_max[:, :, None]), 0.0)
    decay_factor = jnp.exp(prior_max - new_max)
    new_sum = old_sum.T * decay_factor + jnp.sum(exp_scores, axis=-1)
    rounded = exp_scores.astype(jnp.bfloat16)
    contrib = jnp.einsum("hqk,kd->qhd", rounded, value_part, preferred_element_type=jnp.float32)
    new_out = old_out.reshape(rows_here, QHEADS, HEAD) * decay_factor.T[:, :, None] + contrib
    return (new_max.T, new_sum.T, new_out.reshape(rows_here, QHEADS * HEAD))


def in_order(w_ref, my_z):
    parts = []
    for z in range(NZ):
        slot = lax.rem(my_z - z + NZ, NZ)
        for c in range(NC):
            start = pl.multiple_of((c * NZ + slot) * SHARD, SHARD)
            parts.append(w_ref[pl.ds(start, SHARD), :])
    return jnp.concatenate(parts, axis=0)


def finish_kernel(z_ref, att_ref, resid_ref, w_ref, gain_ref, normed_ref, fin_ref, sq_ref):
    step = pl.program_id(0)
    weights = in_order(w_ref, z_ref[0])
    projected = lax.dot_general(
        att_ref[...], weights, (((1,), (1,)), ((), ())), preferred_element_type=jnp.float32
    )
    finished = (resid_ref[...].astype(jnp.float32) + projected).astype(jnp.bfloat16)
    wide = finished.astype(jnp.float32)
    square = wide * wide
    part = sum(square[:, k * HEAD : (k + 1) * HEAD] for k in range(BLOCK // HEAD))

    @pl.when(step == 0)
    def _():
        sq_ref[...] = part

    @pl.when(step > 0)
    def _():
        sq_ref[...] += part

    fin_ref[step] = finished

    @pl.when(step == NY - 1)
    def _():
        total = jnp.sum(sq_ref[...], axis=-1, keepdims=True)
        scale = lax.rsqrt(total / (NY * BLOCK) + 1e-05)
        for k in range(NY):
            cols = slice(k * BLOCK, (k + 1) * BLOCK)
            value = fin_ref[k].astype(jnp.float32) * scale * gain_ref[:, cols]
            normed_ref[:, cols] = value.astype(jnp.bfloat16)


def finish(my_z, attended, resid, weights, gain):
    rows, width = resid.shape
    return pl.pallas_call(
        finish_kernel,
        out_shape=jax.ShapeDtypeStruct((rows, width), jnp.bfloat16),
        grid_spec=pltpu.PrefetchScalarGridSpec(
            num_scalar_prefetch=1,
            grid=(NY,),
            in_specs=[
                pl.BlockSpec((rows, NQ), lambda i, z: (0, 0)),
                pl.BlockSpec((rows, BLOCK), lambda i, z: (0, i)),
                pl.BlockSpec((BLOCK, NQ), lambda i, z: (i, 0)),
                pl.BlockSpec((1, width), lambda i, z: (0, 0)),
            ],
            out_specs=pl.BlockSpec((rows, width), lambda i, z: (0, 0)),
            scratch_shapes=[
                pltpu.VMEM((NY, rows, BLOCK), jnp.bfloat16),
                pltpu.VMEM((rows, HEAD), jnp.float32),
            ],
        ),
        compiler_params=pltpu.CompilerParams(dimension_semantics=("arbitrary",)),
        name="finish",
    )(my_z, attended, resid, weights, gain)


def project_kernel(z_ref, normed_ref, w_ref, query_ref, keyval_ref, acc_ref):
    step = pl.program_id(0)
    weights = in_order(w_ref, z_ref[0])
    part = jnp.dot(normed_ref[...], weights, preferred_element_type=jnp.float32)

    @pl.when(step == 0)
    def _():
        acc_ref[...] = part

    @pl.when(step > 0)
    def _():
        acc_ref[...] += part

    @pl.when(step == NY - 1)
    def _():
        query_ref[...] = acc_ref[:, :NQ].astype(jnp.bfloat16)
        keyval_ref[...] = acc_ref[:, NQ:].astype(jnp.bfloat16)


def project(my_z, normed, weights):
    rows = normed.shape[0]
    return pl.pallas_call(
        project_kernel,
        out_shape=(
            jax.ShapeDtypeStruct((rows, NQ), jnp.bfloat16),
            jax.ShapeDtypeStruct((rows, NKV), jnp.bfloat16),
        ),
        grid_spec=pltpu.PrefetchScalarGridSpec(
            num_scalar_prefetch=1,
            grid=(NY,),
            in_specs=[
                pl.BlockSpec((rows, BLOCK), lambda i, z: (0, i)),
                pl.BlockSpec((BLOCK, NQ + NKV), lambda i, z: (i, 0)),
            ],
            out_specs=(
                pl.BlockSpec((rows, NQ), lambda i, z: (0, 0)),
                pl.BlockSpec((rows, NKV), lambda i, z: (0, 0)),
            ),
            scratch_shapes=[pltpu.VMEM((rows, NQ + NKV), jnp.float32)],
        ),
        compiler_params=pltpu.CompilerParams(dimension_semantics=("arbitrary",)),
        name="project",
    )(my_z, normed, weights)


def per_device(
    resid,
    queries,
    keyvals,
    run_max,
    run_sum,
    run_out,
    span_pair,
    norm_gain,
    w_query,
    w_keyval,
    w_out,
):
    count = NY * NZ * NC
    my_index = lax.axis_index(CTX)
    my_z = lax.axis_index("zl").astype(jnp.int32).reshape(1)
    rows_here = resid.shape[1]
    near_block = lax.ppermute(keyvals[0], CTX, ring(count, -1))
    far_block = lax.ppermute(keyvals[0], CTX, ring(count, -2))

    out_shard = w_out[0].T
    out_parts = [out_shard] + [lax.ppermute(out_shard, "zl", ring(NZ, k)) for k in range(1, NZ)]
    out_rows = lax.all_gather(jnp.concatenate(out_parts), ("y", "c"), axis=0, tiled=True)

    next_shard = jnp.concatenate([w_query[0], w_keyval[0]], axis=1)
    next_parts = []
    for k in range(NZ):
        pairs = [
            (s * NZ + z, (s - 1) % NS * NZ + (z + k) % NZ) for s in range(NS) for z in range(NZ)
        ]
        next_parts.append(lax.ppermute(next_shard, (*SECT, "zl"), pairs))
    gain = lax.ppermute(norm_gain, SECT, ring(NS, -1))
    next_rows = lax.all_gather(jnp.concatenate(next_parts), ("y", "c"), axis=0, tiled=True)

    pos_mine = device_positions(span_pair, my_index, rows_here)
    pos_near = device_positions(span_pair, (my_index + 1) % count, rows_here)
    pos_far = device_positions(span_pair, (my_index + 2) % count, rows_here)
    max_now, sum_now, out_now = flash_step(
        queries[0], far_block, pos_mine, pos_far, run_max[0], run_sum[0], run_out[0]
    )
    max_now, sum_now, out_now = flash_step(
        queries[0], near_block, pos_mine, pos_near, max_now, sum_now, out_now
    )
    divided = out_now.reshape(rows_here, QHEADS, HEAD) / sum_now[:, :, None]
    attended = divided.reshape(rows_here, QHEADS * HEAD).astype(jnp.bfloat16)

    normed = finish(my_z, attended, resid[0], out_rows, gain)
    query_sent, keyval_sent = project(my_z, normed, next_rows)
    keyval_new = lax.ppermute(keyval_sent, SECT, ring(NS, 1))
    query_new = lax.ppermute(query_sent, SECT, ring(NS, 1))

    start_max = jnp.full((rows_here, QHEADS), -1e30, jnp.float32)
    start_sum = jnp.zeros((rows_here, QHEADS), jnp.float32)
    start_out = jnp.zeros((rows_here, QHEADS * HEAD), jnp.float32)
    max_new, sum_new, out_new = flash_step(
        query_new, keyval_new, pos_mine, pos_mine, start_max, start_sum, start_out
    )
    return (query_new[None], keyval_new[None], max_new[None], sum_new[None], out_new[None])


def solution(mesh):
    fine = Mesh(mesh.devices.reshape(2, 4, NY, NZ, NC), (*SECT, *CTX))
    rows = P(SECT, CTX, None)
    return jax.shard_map(
        per_device,
        mesh=fine,
        in_specs=(*[rows] * 6, P(), P(SECT, None), rows, rows, P(SECT, None, CTX)),
        out_specs=(rows,) * 5,
        check_vma=False,
    )
```

```python
import jax
import jax.numpy as jnp
from jax import lax
from jax.experimental import pallas as pl
from jax.experimental.pallas import tpu as pltpu
from jax.sharding import Mesh
from jax.sharding import PartitionSpec as P


HEAD = 128
QHEADS = 4
SECT = ("zh", "x")
CTX = ("y", "zl", "c")
NY, NZ, NC, NS = 8, 4, 2, 8
SHARD = 64
PAIR = 2
NX = 4
CUT = 160
BLOCK = NZ * NC * SHARD
NQ = QHEADS * HEAD
NKV = 2 * HEAD


def ring(count, steps):
    return [(source, (source + steps) % count) for source in range(count)]


def positions(span_ref, device, rows, axis):
    half = rows // 2
    shape = (rows, 1) if axis == 0 else (1, rows)
    offset = lax.broadcasted_iota(jnp.int32, shape, axis)
    first = span_ref[0, device] * half
    second = span_ref[1, device] * half - half
    return offset + jnp.where(offset < half, first, second)


def block_update(query, key, value, keep, old):
    scores = lax.dot_general(
        key, query, (((1,), (1,)), ((), ())), preferred_element_type=jnp.float32
    ) * HEAD ** (-0.5)
    masked = jnp.where(keep, scores, -1e30)
    old_max, old_sum, old_out = old
    new_max = jnp.maximum(old_max, jnp.max(masked, axis=0, keepdims=True))
    exp_scores = jnp.where(keep, jnp.exp(scores - new_max), 0.0)
    decay = jnp.exp(old_max - new_max)
    new_sum = old_sum * decay + jnp.sum(exp_scores, axis=0, keepdims=True)
    contrib = jnp.dot(value, exp_scores.astype(jnp.bfloat16), preferred_element_type=jnp.float32)
    new_out = contrib if old_out is None else old_out * decay + contrib
    return new_max, new_sum, new_out


def attend_kernel(index_ref, span_ref, query_ref, far_ref, near_ref, max_ref, sum_ref, out_ref, att_ref):
    count = NY * NZ * NC
    rows = query_ref.shape[0]
    mine = index_ref[0]
    pos_query = positions(span_ref, mine, rows, 1)
    blocks = []
    for hop, block_ref in ((2, far_ref), (1, near_ref)):
        keep = positions(span_ref, lax.rem(mine + hop, count), rows, 0) <= pos_query
        blocks.append((block_ref[:, :HEAD], block_ref[:, HEAD:].T, keep))
    for h in range(QHEADS):
        cols = slice(h * HEAD, (h + 1) * HEAD)
        state = max_ref[h : h + 1, :], sum_ref[h : h + 1, :], out_ref[:, cols].T
        for block in blocks:
            state = block_update(query_ref[:, cols], *block, state)
        att_ref[:, cols] = (state[2] / state[1]).T.astype(jnp.bfloat16)


def attend(my_index, spans, *operands):
    return pl.pallas_call(
        attend_kernel,
        out_shape=jax.ShapeDtypeStruct(operands[0].shape, jnp.bfloat16),
        in_specs=[pl.BlockSpec(memory_space=pltpu.SMEM)] * 2
        + [pl.BlockSpec(memory_space=pltpu.VMEM)] * len(operands),
        out_specs=pl.BlockSpec(memory_space=pltpu.VMEM),
        name="attend",
    )(my_index, spans, *operands)


def in_order(w_ref, base, slots):
    parts = []
    for z in range(NZ):
        for c in range(NC):
            start = base + (c * NZ + slots[z]) * SHARD
            if not isinstance(start, int):
                start = pl.multiple_of(start, SHARD)
            parts.append(w_ref[pl.ds(start, SHARD), :])
    return parts


def layer_kernel(
    place_ref,
    span_ref,
    att_ref,
    direct_ref,
    near_ref,
    far_ref,
    gain_ref,
    out_a_ref,
    out_b_ref,
    next_ref,
    query_ref,
    keyval_ref,
    max_ref,
    sum_ref,
    wide_ref,
    rows_ref,
    sq_ref,
    acc_ref,
):
    step = pl.program_id(0)
    half = NY // PAIR
    width = PAIR * BLOCK

    @pl.when(step < half)
    def _():
        slots = [lax.rem(place_ref[1] - z + NZ, NZ) for z in range(NZ)]

        def part(w_ref, cols):
            pieces = []
            for k in range(PAIR):
                pieces += in_order(w_ref, k * BLOCK, slots)
            return lax.dot_general(
                att_ref[:, cols],
                jnp.concatenate(pieces, axis=0),
                (((1,), (1,)), ((), ())),
                preferred_element_type=jnp.float32,
            )

        projected = part(out_a_ref, slice(0, NQ // 2)) + part(out_b_ref, slice(NQ // 2, NQ))
        by_near = place_ref[2] > 0
        routed = jnp.where(by_near, near_ref[...], far_ref[...])
        resid = jnp.concatenate([direct_ref[...], routed], axis=0)
        finished = (resid.astype(jnp.float32) + projected).astype(jnp.bfloat16)
        square = finished.astype(jnp.float32)
        square = square * square
        total = sum(square[:, j * HEAD : (j + 1) * HEAD] for j in range(width // HEAD))
        rows_ref[step] = finished

        @pl.when(step == 0)
        def _():
            sq_ref[...] = total

        @pl.when(step > 0)
        def _():
            sq_ref[...] += total

    @pl.when(step == half - 1)
    def _():
        mean = jnp.sum(sq_ref[...], axis=-1, keepdims=True) / (NY * BLOCK)
        scale = lax.rsqrt(mean + 1e-05)
        for k in range(half):
            gain = gain_ref[:, k * width : (k + 1) * width]
            value = rows_ref[k].astype(jnp.float32) * scale * gain
            rows_ref[k] = value.astype(jnp.bfloat16)

    @pl.when(step >= half)
    def _():
        pieces = []
        for k in range(PAIR):
            pieces += in_order(next_ref, k * BLOCK, range(NZ))
        total = jnp.dot(
            rows_ref[step - half],
            jnp.concatenate(pieces, axis=0),
            preferred_element_type=jnp.float32,
        )

        @pl.when(step == half)
        def _():
            acc_ref[...] = total

        @pl.when(step > half)
        def _():
            acc_ref[...] += total

    @pl.when(step == 2 * half - 1)
    def _():
        rows = query_ref.shape[0]
        query_ref[...] = acc_ref[:, :NQ].astype(jnp.bfloat16)
        keyval_ref[...] = acc_ref[:, NQ:].astype(jnp.bfloat16)
        mine = place_ref[0]
        keep = positions(span_ref, mine, rows, 0) <= positions(span_ref, mine, rows, 1)
        key = keyval_ref[:, :HEAD]
        value = keyval_ref[:, HEAD:].T
        for h in range(QHEADS):
            cols = slice(h * HEAD, (h + 1) * HEAD)
            state = jnp.full((1, rows), -1e30, jnp.float32), jnp.zeros((1, rows), jnp.float32), None
            state = block_update(query_ref[:, cols], key, value, keep, state)
            max_ref[h : h + 1, :] = state[0]
            sum_ref[h : h + 1, :] = state[1]
            wide_ref[:, cols] = state[2].T


def layer(place, spans, attended, direct, near, far, gain, weights):
    rows = attended.shape[0]
    half = NY // PAIR
    width = PAIR * BLOCK
    first = lambda i: jnp.minimum(i, half - 1)
    second = lambda i: jnp.maximum(i - half, 0)
    whole = lambda shape: pl.BlockSpec(shape, lambda i, *_: (0,) * len(shape))
    by_cols = lambda v: pl.BlockSpec((v.shape[0], width), lambda i, *_: (0, first(i)))
    out_cols = (NQ + NKV) // (NQ // 2)
    stat = jax.ShapeDtypeStruct((QHEADS, rows), jnp.float32)
    out_shape = (
        jax.ShapeDtypeStruct((rows, NQ), jnp.bfloat16),
        jax.ShapeDtypeStruct((rows, NKV), jnp.bfloat16),
        stat,
        stat,
        jax.ShapeDtypeStruct((rows, NQ), jnp.float32),
    )
    return pl.pallas_call(
        layer_kernel,
        out_shape=out_shape,
        grid_spec=pltpu.PrefetchScalarGridSpec(
            num_scalar_prefetch=2,
            grid=(2 * half,),
            in_specs=[
                whole(attended.shape),
                by_cols(direct),
                by_cols(near),
                by_cols(far),
                whole(gain.shape),
                pl.BlockSpec((width, NQ // 2), lambda i, *_: (first(i), out_cols)),
                pl.BlockSpec((width, NQ // 2), lambda i, *_: (first(i), out_cols + 1)),
                pl.BlockSpec((width, NQ + NKV), lambda i, *_: (second(i), 0)),
            ],
            out_specs=tuple(whole(v.shape) for v in out_shape),
            scratch_shapes=[
                pltpu.VMEM((half, rows, width), jnp.bfloat16),
                pltpu.VMEM((rows, HEAD), jnp.float32),
                pltpu.VMEM((rows, NQ + NKV), jnp.float32),
            ],
        ),
        compiler_params=pltpu.CompilerParams(dimension_semantics=("arbitrary",)),
        name="layer",
    )(place, spans, attended, direct, near, far, gain, weights, weights, weights)


def per_device(
    resid,
    queries,
    keyvals,
    run_max,
    run_sum,
    run_out,
    span_pair,
    norm_gain,
    w_query,
    w_keyval,
    w_out,
):
    count = NY * NZ * NC
    my_index = lax.axis_index(CTX).astype(jnp.int32)
    my_z = lax.axis_index("zl").astype(jnp.int32)
    my_x = lax.axis_index("x").astype(jnp.int32)
    spans = span_pair.T

    out_parts = []
    for k in range(NZ):
        pairs = [
            (s * NZ + z, (s + 1) % NS * NZ + (z + k) % NZ) for s in range(NS) for z in range(NZ)
        ]
        out_parts.append(lax.ppermute(w_out[0].T, (*SECT, "zl"), pairs))
    near_block = lax.ppermute(keyvals[0], CTX, ring(count, -1))
    far_block = lax.ppermute(keyvals[0], CTX, ring(count, -2))

    next_shard = jnp.concatenate([w_query[0], w_keyval[0]], axis=1)
    next_copies = jnp.broadcast_to(next_shard, (NZ, SHARD, NQ + NKV))
    next_rows = lax.all_to_all(next_copies, "zl", 0, 0, tiled=True).reshape(NZ * SHARD, NQ + NKV)
    shards = jnp.concatenate([next_rows, jnp.concatenate(out_parts)], axis=1)
    weights = lax.all_gather(shards, ("y", "c"), axis=0, tiled=True)

    rest = resid[0, CUT:]
    wrap = NX - 1
    turn = [(s, s + 1) for s in range(NS) if s % NX < wrap - 1]
    turn += [(s, (s + NX) % NS) for s in range(NS) if s % NX == wrap]
    near = lax.ppermute(rest, SECT, turn)
    direct = lax.ppermute(resid[0, :CUT], SECT, ring(NS, 1))
    attended = attend(
        my_index.reshape(1), spans, queries[0], far_block, near_block,
        run_max[0].T, run_sum[0].T, run_out[0],
    )
    attended_sent = lax.ppermute(attended, SECT, ring(NS, 1))
    near, _ = lax.optimization_barrier((near, attended))
    leave = [(s, (s + 1) % NX + s // NX * NX) for s in range(NS) if s % NX >= wrap - 1]
    leaving = jnp.where(my_x == wrap, near, rest)
    far = lax.ppermute(leaving, SECT, leave)
    by_near = ((my_x > 0) & (my_x < wrap)).astype(jnp.int32)
    place = jnp.stack([my_index, my_z, by_near])
    query_new, keyval_new, max_new, sum_new, out_new = layer(
        place, spans, attended_sent, direct, near, far, norm_gain, weights
    )
    return (query_new[None], keyval_new[None], max_new.T[None], sum_new.T[None], out_new[None])


def solution(mesh):
    fine = Mesh(mesh.devices.reshape(2, NX, NY, NZ, NC), (*SECT, *CTX))
    rows = P(SECT, CTX, None)
    return jax.shard_map(
        per_device,
        mesh=fine,
        in_specs=(*[rows] * 6, P(), P(SECT, None), rows, rows, P(SECT, None, CTX)),
        out_specs=(rows,) * 5,
        check_vma=False,
    )
```

```python
import jax
import jax.numpy as jnp
from jax import lax
from jax.experimental import pallas as pl
from jax.experimental.pallas import tpu as pltpu
from jax.sharding import Mesh
from jax.sharding import PartitionSpec as P


HEAD = 128
QHEADS = 4
SECT = ("zh", "x")
CTX = ("y", "zl", "c")
NY, NZ, NC, NS = 8, 4, 2, 8
SHARD = 64
PAIR = 2
NX = 4
CUT = 144
BLOCK = NZ * NC * SHARD
NQ = QHEADS * HEAD
NKV = 2 * HEAD


def ring(count, steps):
    return [(source, (source + steps) % count) for source in range(count)]


def positions(span_ref, device, rows, axis):
    half = rows // 2
    shape = (rows, 1) if axis == 0 else (1, rows)
    offset = lax.broadcasted_iota(jnp.int32, shape, axis)
    first = span_ref[0, device] * half
    second = span_ref[1, device] * half - half
    return offset + jnp.where(offset < half, first, second)


def block_update(query, key, value, keep, old):
    scores = lax.dot_general(
        key, query, (((1,), (1,)), ((), ())), preferred_element_type=jnp.float32
    ) * HEAD ** (-0.5)
    masked = jnp.where(keep, scores, -1e30)
    old_max, old_sum, old_out = old
    new_max = jnp.maximum(old_max, jnp.max(masked, axis=0, keepdims=True))
    exp_scores = jnp.where(keep, jnp.exp(scores - new_max), 0.0)
    decay = jnp.exp(old_max - new_max)
    new_sum = old_sum * decay + jnp.sum(exp_scores, axis=0, keepdims=True)
    contrib = jnp.dot(value, exp_scores.astype(jnp.bfloat16), preferred_element_type=jnp.float32)
    new_out = contrib if old_out is None else old_out * decay + contrib
    return new_max, new_sum, new_out


def attend_kernel(index_ref, span_ref, query_ref, far_ref, near_ref, max_ref, sum_ref, out_ref, att_ref):
    count = NY * NZ * NC
    rows = query_ref.shape[0]
    mine = index_ref[0]
    pos_query = positions(span_ref, mine, rows, 1)
    blocks = []
    for hop, block_ref in ((2, far_ref), (1, near_ref)):
        keep = positions(span_ref, lax.rem(mine + hop, count), rows, 0) <= pos_query
        blocks.append((block_ref[:, :HEAD], block_ref[:, HEAD:].T, keep))
    for h in range(QHEADS):
        cols = slice(h * HEAD, (h + 1) * HEAD)
        state = max_ref[h : h + 1, :], sum_ref[h : h + 1, :], out_ref[:, cols].T
        for block in blocks:
            state = block_update(query_ref[:, cols], *block, state)
        att_ref[:, cols] = (state[2] / state[1]).T.astype(jnp.bfloat16)


def attend(my_index, spans, *operands):
    return pl.pallas_call(
        attend_kernel,
        out_shape=jax.ShapeDtypeStruct(operands[0].shape, jnp.bfloat16),
        in_specs=[pl.BlockSpec(memory_space=pltpu.SMEM)] * 2
        + [pl.BlockSpec(memory_space=pltpu.VMEM)] * len(operands),
        out_specs=pl.BlockSpec(memory_space=pltpu.VMEM),
        name="attend",
    )(my_index, spans, *operands)


def in_order(w_ref):
    parts = []
    for y in range(w_ref.shape[0] // BLOCK):
        for z in range(NZ):
            for c in range(NC):
                start = ((y * NC + c) * NZ + z) * SHARD
                parts.append(w_ref[start : start + SHARD, :])
    return jnp.concatenate(parts, axis=0)


def layer_kernel(
    place_ref,
    span_ref,
    att_ref,
    direct_ref,
    near_ref,
    far_ref,
    gain_ref,
    out_a_ref,
    out_b_ref,
    next_ref,
    query_ref,
    keyval_ref,
    max_ref,
    sum_ref,
    wide_ref,
    rows_ref,
    sq_ref,
    acc_ref,
):
    step = pl.program_id(0)
    half = NY // PAIR
    width = PAIR * BLOCK

    @pl.when(step < half)
    def _():
        def part(w_ref, cols):
            return lax.dot_general(
                att_ref[:, cols],
                in_order(w_ref),
                (((1,), (1,)), ((), ())),
                preferred_element_type=jnp.float32,
            )

        projected = part(out_a_ref, slice(0, NQ // 2)) + part(out_b_ref, slice(NQ // 2, NQ))
        by_near = place_ref[1] > 0
        routed = jnp.where(by_near, near_ref[...], far_ref[...])
        resid = jnp.concatenate([direct_ref[...], routed], axis=0)
        finished = (resid.astype(jnp.float32) + projected).astype(jnp.bfloat16)
        square = finished.astype(jnp.float32)
        square = square * square
        total = sum(square[:, j * HEAD : (j + 1) * HEAD] for j in range(width // HEAD))
        rows_ref[step] = finished

        @pl.when(step == 0)
        def _():
            sq_ref[...] = total

        @pl.when(step > 0)
        def _():
            sq_ref[...] += total

    @pl.when(step == half - 1)
    def _():
        mean = jnp.sum(sq_ref[...], axis=-1, keepdims=True) / (NY * BLOCK)
        scale = lax.rsqrt(mean + 1e-05)
        for k in range(half):
            gain = gain_ref[:, k * width : (k + 1) * width]
            value = rows_ref[k].astype(jnp.float32) * scale * gain
            rows_ref[k] = value.astype(jnp.bfloat16)

    @pl.when(step >= half)
    def _():
        total = jnp.dot(
            rows_ref[step - half], in_order(next_ref), preferred_element_type=jnp.float32
        )

        @pl.when(step == half)
        def _():
            acc_ref[...] = total

        @pl.when(step > half)
        def _():
            acc_ref[...] += total

    @pl.when(step == 2 * half - 1)
    def _():
        rows = query_ref.shape[0]
        query_ref[...] = acc_ref[:, :NQ].astype(jnp.bfloat16)
        keyval_ref[...] = acc_ref[:, NQ:].astype(jnp.bfloat16)
        mine = place_ref[0]
        keep = positions(span_ref, mine, rows, 0) <= positions(span_ref, mine, rows, 1)
        key = keyval_ref[:, :HEAD]
        value = keyval_ref[:, HEAD:].T
        for h in range(QHEADS):
            cols = slice(h * HEAD, (h + 1) * HEAD)
            state = jnp.full((1, rows), -1e30, jnp.float32), jnp.zeros((1, rows), jnp.float32), None
            state = block_update(query_ref[:, cols], key, value, keep, state)
            max_ref[h : h + 1, :] = state[0]
            sum_ref[h : h + 1, :] = state[1]
            wide_ref[:, cols] = state[2].T


def layer(place, spans, attended, direct, near, far, gain, weights):
    rows = attended.shape[0]
    half = NY // PAIR
    width = PAIR * BLOCK
    first = lambda i: jnp.minimum(i, half - 1)
    second = lambda i: jnp.maximum(i - half, 0)
    whole = lambda shape: pl.BlockSpec(shape, lambda i, *_: (0,) * len(shape))
    by_cols = lambda v: pl.BlockSpec((v.shape[0], width), lambda i, *_: (0, first(i)))
    out_cols = (NQ + NKV) // (NQ // 2)
    stat = jax.ShapeDtypeStruct((QHEADS, rows), jnp.float32)
    out_shape = (
        jax.ShapeDtypeStruct((rows, NQ), jnp.bfloat16),
        jax.ShapeDtypeStruct((rows, NKV), jnp.bfloat16),
        stat,
        stat,
        jax.ShapeDtypeStruct((rows, NQ), jnp.float32),
    )
    return pl.pallas_call(
        layer_kernel,
        out_shape=out_shape,
        grid_spec=pltpu.PrefetchScalarGridSpec(
            num_scalar_prefetch=2,
            grid=(2 * half,),
            in_specs=[
                whole(attended.shape),
                by_cols(direct),
                by_cols(near),
                by_cols(far),
                whole(gain.shape),
                pl.BlockSpec((width, NQ // 2), lambda i, *_: (first(i), out_cols)),
                pl.BlockSpec((width, NQ // 2), lambda i, *_: (first(i), out_cols + 1)),
                pl.BlockSpec((width, NQ + NKV), lambda i, *_: (second(i), 0)),
            ],
            out_specs=tuple(whole(v.shape) for v in out_shape),
            scratch_shapes=[
                pltpu.VMEM((half, rows, width), jnp.bfloat16),
                pltpu.VMEM((rows, HEAD), jnp.float32),
                pltpu.VMEM((rows, NQ + NKV), jnp.float32),
            ],
        ),
        compiler_params=pltpu.CompilerParams(dimension_semantics=("arbitrary",)),
        name="layer",
    )(place, spans, attended, direct, near, far, gain, weights, weights, weights)


def per_device(
    resid,
    queries,
    keyvals,
    run_max,
    run_sum,
    run_out,
    span_pair,
    norm_gain,
    w_query,
    w_keyval,
    w_out,
):
    count = NY * NZ * NC
    my_index = lax.axis_index(CTX).astype(jnp.int32)
    my_x = lax.axis_index("x").astype(jnp.int32)
    spans = span_pair.T

    out_shard = lax.ppermute(w_out[0].T, SECT, ring(NS, 1))
    next_shard = jnp.concatenate([w_query[0], w_keyval[0]], axis=1)

    def along_z(shard):
        copies = jnp.broadcast_to(shard, (NZ, *shard.shape))
        return lax.all_to_all(copies, "zl", 0, 0, tiled=True).reshape(NZ * SHARD, -1)

    next_rows = along_z(next_shard)
    out_rows = along_z(out_shard)
    shards = jnp.concatenate([next_rows, out_rows], axis=1)
    weights = lax.all_gather(shards, ("y", "c"), axis=0, tiled=True)

    turn = [(s, (s + 1) % NX + s // NX * NX) for s in range(NS)]
    near = lax.ppermute(resid[0, CUT:], SECT, turn)
    direct = lax.ppermute(resid[0, :CUT], SECT, ring(NS, 1))
    near_block = lax.ppermute(keyvals[0], CTX, ring(count, -1))
    far_block = lax.ppermute(keyvals[0], CTX, ring(count, -2))
    attended = attend(
        my_index.reshape(1), spans, queries[0], far_block, near_block,
        run_max[0].T, run_sum[0].T, run_out[0],
    )
    attended_sent = lax.ppermute(attended, SECT, ring(NS, 1))
    leaving, _ = lax.optimization_barrier((near, attended))
    far = lax.ppermute(leaving, SECT, [(0, NX), (NX, 0)])
    place = jnp.stack([my_index, (my_x > 0).astype(jnp.int32)])
    query_new, keyval_new, max_new, sum_new, out_new = layer(
        place, spans, attended_sent, direct, near, far, norm_gain, weights
    )
    return (query_new[None], keyval_new[None], max_new.T[None], sum_new.T[None], out_new[None])


def solution(mesh):
    fine = Mesh(mesh.devices.reshape(2, NX, NY, NZ, NC), (*SECT, *CTX))
    rows = P(SECT, CTX, None)
    return jax.shard_map(
        per_device,
        mesh=fine,
        in_specs=(*[rows] * 6, P(), P(SECT, None), rows, rows, P(SECT, None, CTX)),
        out_specs=(rows,) * 5,
        check_vma=False,
    )
```

```python
import jax
import jax.numpy as jnp
from jax import lax
from jax.experimental import pallas as pl
from jax.experimental.pallas import tpu as pltpu
from jax.sharding import Mesh
from jax.sharding import PartitionSpec as P


HEAD = 128
QHEADS = 4
SECT = ("zh", "x")
CTX = ("y", "zl", "c")
NY, NZ, NC, NS = 8, 4, 2, 8
SHARD = 64
NX = 4
STARTS = (0, 128, 192)
BLOCK = NZ * NC * SHARD
NQ = QHEADS * HEAD
NKV = 2 * HEAD


def ring(count, steps):
    return [(source, (source + steps) % count) for source in range(count)]


def positions(span_ref, device, rows, axis):
    half = rows // 2
    shape = (rows, 1) if axis == 0 else (1, rows)
    offset = lax.broadcasted_iota(jnp.int32, shape, axis)
    first = span_ref[0, device] * half
    second = span_ref[1, device] * half - half
    return offset + jnp.where(offset < half, first, second)


def block_update(query, key, value, keep, old):
    scores = lax.dot_general(
        key, query, (((1,), (1,)), ((), ())), preferred_element_type=jnp.float32
    ) * HEAD ** (-0.5)
    masked = jnp.where(keep, scores, -1e30)
    old_max, old_sum, old_out = old
    new_max = jnp.maximum(old_max, jnp.max(masked, axis=0, keepdims=True))
    exp_scores = jnp.exp(masked - new_max)
    decay = jnp.exp(old_max - new_max)
    new_sum = old_sum * decay + jnp.sum(exp_scores, axis=0, keepdims=True)
    contrib = jnp.dot(value, exp_scores.astype(jnp.bfloat16), preferred_element_type=jnp.float32)
    new_out = contrib if old_out is None else old_out * decay + contrib
    return new_max, new_sum, new_out


def attend_kernel(index_ref, span_ref, query_ref, far_ref, near_ref, max_ref, sum_ref, out_ref, att_ref):
    count = NY * NZ * NC
    rows = query_ref.shape[0]
    mine = index_ref[0]
    pos_query = positions(span_ref, mine, rows, 1)
    blocks = []
    for hop, block_ref in ((2, far_ref), (1, near_ref)):
        keep = positions(span_ref, lax.rem(mine + hop, count), rows, 0) <= pos_query
        blocks.append((block_ref[:, :HEAD], block_ref[:, HEAD:].T, keep))
    for h in range(QHEADS):
        cols = slice(h * HEAD, (h + 1) * HEAD)
        state = max_ref[h : h + 1, :], sum_ref[h : h + 1, :], out_ref[:, cols].T
        for block in blocks:
            state = block_update(query_ref[:, cols], *block, state)
        att_ref[:, cols] = (state[2] / state[1]).T.astype(jnp.bfloat16)


def attend(my_index, spans, *operands):
    return pl.pallas_call(
        attend_kernel,
        out_shape=jax.ShapeDtypeStruct(operands[0].shape, jnp.bfloat16),
        in_specs=[pl.BlockSpec(memory_space=pltpu.SMEM)] * 2
        + [pl.BlockSpec(memory_space=pltpu.VMEM)] * len(operands),
        out_specs=pl.BlockSpec(memory_space=pltpu.VMEM),
        name="attend",
    )(my_index, spans, *operands)


def in_order(w_ref, y, cols):
    parts = []
    for z in range(NZ):
        for c in range(NC):
            start = ((y * NC + c) * NZ + z) * SHARD
            parts.append(w_ref[start : start + SHARD, cols])
    return jnp.concatenate(parts, axis=0)


def layer_kernel(
    place_ref,
    span_ref,
    att_ref,
    gain_ref,
    direct_ref,
    near_a_ref,
    near_b_ref,
    far_a_ref,
    far_b_ref,
    weight_ref,
    query_ref,
    keyval_ref,
    max_ref,
    sum_ref,
    wide_ref,
    resid_ref,
    out_ref,
    row_sems,
    out_sems,
):
    rows = query_ref.shape[0]
    by_near = place_ref[1] > 0

    def out_copy(y):
        block = pl.ds(y * BLOCK, BLOCK)
        return pltpu.make_async_copy(weight_ref.at[block, :], out_ref.at[block, :], out_sems.at[y])

    def row_copy(source, part):
        block = resid_ref.at[pl.ds(STARTS[part], source.shape[0]), :]
        return pltpu.make_async_copy(source, block, row_sems.at[part])

    out_copy(0).start()
    row_copy(direct_ref, 0).start()

    @pl.when(by_near)
    def _():
        row_copy(near_a_ref, 1).start()
        row_copy(near_b_ref, 2).start()

    @pl.when(jnp.logical_not(by_near))
    def _():
        row_copy(far_a_ref, 1).start()
        row_copy(far_b_ref, 2).start()

    for y in range(1, NY):
        out_copy(y).start()
    for part, source in enumerate((direct_ref, near_a_ref, near_b_ref)):
        row_copy(source, part).wait()

    total = None
    for y in range(NY):
        cols = slice(y * BLOCK, (y + 1) * BLOCK)
        out_copy(y).wait()
        projected = lax.dot_general(
            att_ref[...],
            in_order(out_ref, y, slice(NQ + NKV, None)),
            (((1,), (1,)), ((), ())),
            preferred_element_type=jnp.float32,
        )
        finished = (resid_ref[:, cols].astype(jnp.float32) + projected).astype(jnp.bfloat16)
        square = finished.astype(jnp.float32)
        square = square * square
        part = sum(square[:, j * HEAD : (j + 1) * HEAD] for j in range(BLOCK // HEAD))
        total = part if total is None else total + part
        resid_ref[:, cols] = finished

    scale = lax.rsqrt(jnp.sum(total, axis=-1, keepdims=True) / (NY * BLOCK) + 1e-05)
    total = None
    for y in range(NY):
        cols = slice(y * BLOCK, (y + 1) * BLOCK)
        value = resid_ref[:, cols].astype(jnp.float32) * scale * gain_ref[:, cols]
        part = jnp.dot(
            value.astype(jnp.bfloat16), in_order(out_ref, y, slice(0, NQ + NKV)), preferred_element_type=jnp.float32
        )
        total = part if total is None else total + part

    query = total[:, :NQ].astype(jnp.bfloat16)
    keyval = total[:, NQ:].astype(jnp.bfloat16)
    query_ref[...] = query
    keyval_ref[...] = keyval
    mine = place_ref[0]
    keep = positions(span_ref, mine, rows, 0) <= positions(span_ref, mine, rows, 1)
    key = keyval[:, :HEAD]
    value = keyval[:, HEAD:].T
    for h in range(QHEADS):
        cols = slice(h * HEAD, (h + 1) * HEAD)
        state = jnp.full((1, rows), -1e30, jnp.float32), jnp.zeros((1, rows), jnp.float32), None
        state = block_update(query[:, cols], key, value, keep, state)
        max_ref[h : h + 1, :] = state[0]
        sum_ref[h : h + 1, :] = state[1]
        wide_ref[:, cols] = state[2].T


def layer(place, spans, attended, gain, parts, weights):
    rows = attended.shape[0]
    depth = weights.shape[0]
    smem = pl.BlockSpec(memory_space=pltpu.SMEM)
    vmem = pl.BlockSpec(memory_space=pltpu.VMEM)
    anywhere = pl.BlockSpec(memory_space=pl.ANY)
    stat = jax.ShapeDtypeStruct((QHEADS, rows), jnp.float32)
    return pl.pallas_call(
        layer_kernel,
        out_shape=(
            jax.ShapeDtypeStruct((rows, NQ), jnp.bfloat16),
            jax.ShapeDtypeStruct((rows, NKV), jnp.bfloat16),
            stat,
            stat,
            jax.ShapeDtypeStruct((rows, NQ), jnp.float32),
        ),
        in_specs=[smem, smem, vmem, vmem] + [anywhere] * (len(parts) + 1),
        out_specs=(vmem,) * 5,
        scratch_shapes=[
            pltpu.VMEM((rows, depth), jnp.bfloat16),
            pltpu.VMEM(weights.shape, jnp.bfloat16),
            pltpu.SemaphoreType.DMA((len(STARTS),)),
            pltpu.SemaphoreType.DMA((NY,)),
        ],
        name="layer",
    )(place, spans, attended, gain, *parts, weights)


def per_device(
    resid,
    queries,
    keyvals,
    run_max,
    run_sum,
    run_out,
    span_pair,
    norm_gain,
    w_query,
    w_keyval,
    w_out,
):
    count = NY * NZ * NC
    my_index = lax.axis_index(CTX).astype(jnp.int32)
    my_x = lax.axis_index("x").astype(jnp.int32)
    spans = span_pair.T

    out_shard = lax.ppermute(w_out[0].T, SECT, ring(NS, 1))
    next_shard = jnp.concatenate([w_query[0], w_keyval[0]], axis=1)

    def along_z(shard):
        copies = jnp.broadcast_to(shard, (NZ, *shard.shape))
        return lax.all_to_all(copies, "zl", 0, 0, tiled=True).reshape(NZ * SHARD, -1)

    next_rows = along_z(next_shard)
    out_rows = along_z(out_shard)
    shards = jnp.concatenate([next_rows, out_rows], axis=1)
    weights = lax.all_gather(shards, ("y", "c"), axis=0, tiled=True)

    turn = [(s, (s + 1) % NX + s // NX * NX) for s in range(NS)]
    near_a = lax.ppermute(resid[0, STARTS[1] : STARTS[2]], SECT, turn)
    direct = lax.ppermute(resid[0, : STARTS[1]], SECT, ring(NS, 1))
    near_b = lax.ppermute(resid[0, STARTS[2] :], SECT, turn)
    near_block = lax.ppermute(keyvals[0], CTX, ring(count, -1))
    far_block = lax.ppermute(keyvals[0], CTX, ring(count, -2))
    attended = attend(
        my_index.reshape(1), spans, queries[0], far_block, near_block,
        run_max[0].T, run_sum[0].T, run_out[0],
    )
    attended_sent = lax.ppermute(attended, SECT, ring(NS, 1))
    far_a = lax.ppermute(near_a, SECT, [(0, NX), (NX, 0)])
    leaving_b, far_a = lax.optimization_barrier((near_b, far_a))
    far_b = lax.ppermute(leaving_b, SECT, [(0, NX), (NX, 0)])
    place = jnp.stack([my_index, (my_x > 0).astype(jnp.int32)])
    query_new, keyval_new, max_new, sum_new, out_new = layer(
        place, spans, attended_sent, norm_gain, (direct, near_a, near_b, far_a, far_b), weights
    )
    return (query_new[None], keyval_new[None], max_new.T[None], sum_new.T[None], out_new[None])


def solution(mesh):
    fine = Mesh(mesh.devices.reshape(2, NX, NY, NZ, NC), (*SECT, *CTX))
    rows = P(SECT, CTX, None)
    return jax.shard_map(
        per_device,
        mesh=fine,
        in_specs=(*[rows] * 6, P(), P(SECT, None), rows, rows, P(SECT, None, CTX)),
        out_specs=(rows,) * 5,
        check_vma=False,
    )
```

```python
import jax
import jax.numpy as jnp
from jax import lax
from jax.experimental import pallas as pl
from jax.experimental.pallas import tpu as pltpu
from jax.sharding import Mesh
from jax.sharding import PartitionSpec as P


HEAD = 128
QHEADS = 4
SECT = ("zh", "x")
CTX = ("y", "zl", "c")
NY, NZ, NC, NS = 8, 4, 2, 8
SHARD = 64
NX = 4
STARTS = (0, 96, 176)
BLOCK = NZ * NC * SHARD
NQ = QHEADS * HEAD
NKV = 2 * HEAD


def ring(count, steps):
    return [(source, (source + steps) % count) for source in range(count)]


def positions(span_ref, device, rows, axis):
    half = rows // 2
    shape = (rows, 1) if axis == 0 else (1, rows)
    offset = lax.broadcasted_iota(jnp.int32, shape, axis)
    first = span_ref[0, device] * half
    second = span_ref[1, device] * half - half
    return offset + jnp.where(offset < half, first, second)


def block_update(query, key, value, keep, old):
    scores = lax.dot_general(
        key, query, (((1,), (1,)), ((), ())), preferred_element_type=jnp.float32
    ) * HEAD ** (-0.5)
    masked = jnp.where(keep, scores, -1e30)
    old_max, old_sum, old_out = old
    new_max = jnp.maximum(old_max, jnp.max(masked, axis=0, keepdims=True))
    exp_scores = jnp.exp(masked - new_max)
    decay = jnp.exp(old_max - new_max)
    new_sum = old_sum * decay + jnp.sum(exp_scores, axis=0, keepdims=True)
    contrib = jnp.dot(value, exp_scores.astype(jnp.bfloat16), preferred_element_type=jnp.float32)
    new_out = contrib if old_out is None else old_out * decay + contrib
    return new_max, new_sum, new_out


def attend_kernel(index_ref, span_ref, query_ref, far_ref, near_ref, max_ref, sum_ref, out_ref, att_ref):
    count = NY * NZ * NC
    rows = query_ref.shape[0]
    mine = index_ref[0]
    pos_query = positions(span_ref, mine, rows, 1)
    blocks = []
    for hop, block_ref in ((2, far_ref), (1, near_ref)):
        keep = positions(span_ref, lax.rem(mine + hop, count), rows, 0) <= pos_query
        blocks.append((block_ref[:, :HEAD], block_ref[:, HEAD:].T, keep))
    for h in range(QHEADS):
        cols = slice(h * HEAD, (h + 1) * HEAD)
        state = max_ref[h : h + 1, :], sum_ref[h : h + 1, :], out_ref[:, cols].T
        for block in blocks:
            state = block_update(query_ref[:, cols], *block, state)
        att_ref[:, cols] = (state[2] / state[1]).T.astype(jnp.bfloat16)


def attend(my_index, spans, *operands):
    return pl.pallas_call(
        attend_kernel,
        out_shape=jax.ShapeDtypeStruct(operands[0].shape, jnp.bfloat16),
        in_specs=[pl.BlockSpec(memory_space=pltpu.SMEM)] * 2
        + [pl.BlockSpec(memory_space=pltpu.VMEM)] * len(operands),
        out_specs=pl.BlockSpec(memory_space=pltpu.VMEM),
        name="attend",
    )(my_index, spans, *operands)


def in_order(w_ref, y, cols):
    parts = []
    for z in range(NZ):
        for c in range(NC):
            start = ((y * NC + c) * NZ + z) * SHARD
            parts.append(w_ref[start : start + SHARD, cols])
    return jnp.concatenate(parts, axis=0)


def layer_kernel(
    place_ref,
    span_ref,
    att_ref,
    gain_ref,
    direct_ref,
    near_ref,
    far_ref,
    first_ref,
    second_ref,
    weight_ref,
    query_ref,
    keyval_ref,
    max_ref,
    sum_ref,
    wide_ref,
    resid_ref,
    out_ref,
    row_sems,
    out_sems,
):
    rows = query_ref.shape[0]

    def out_copy(y):
        block = pl.ds(y * BLOCK, BLOCK)
        return pltpu.make_async_copy(weight_ref.at[block, :], out_ref.at[block, :], out_sems.at[y])

    def row_copy(source, part):
        block = resid_ref.at[pl.ds(STARTS[part], source.shape[0]), :]
        return pltpu.make_async_copy(source, block, row_sems.at[part])

    out_copy(0).start()
    row_copy(direct_ref, 0).start()

    for part, one, other in ((1, near_ref, far_ref), (2, first_ref, second_ref)):
        chosen = place_ref[part] > 0

        @pl.when(chosen)
        def _():
            row_copy(one, part).start()

        @pl.when(jnp.logical_not(chosen))
        def _():
            row_copy(other, part).start()

    for y in range(1, NY):
        out_copy(y).start()
    for part, source in enumerate((direct_ref, near_ref, first_ref)):
        row_copy(source, part).wait()

    total = None
    for y in range(NY):
        cols = slice(y * BLOCK, (y + 1) * BLOCK)
        out_copy(y).wait()
        projected = lax.dot_general(
            att_ref[...],
            in_order(out_ref, y, slice(NQ + NKV, None)),
            (((1,), (1,)), ((), ())),
            preferred_element_type=jnp.float32,
        )
        finished = (resid_ref[:, cols].astype(jnp.float32) + projected).astype(jnp.bfloat16)
        square = finished.astype(jnp.float32)
        square = square * square
        part = sum(square[:, j * HEAD : (j + 1) * HEAD] for j in range(BLOCK // HEAD))
        total = part if total is None else total + part
        resid_ref[:, cols] = finished

    scale = lax.rsqrt(jnp.sum(total, axis=-1, keepdims=True) / (NY * BLOCK) + 1e-05)
    total = None
    for y in range(NY):
        cols = slice(y * BLOCK, (y + 1) * BLOCK)
        value = resid_ref[:, cols].astype(jnp.float32) * scale * gain_ref[:, cols]
        part = jnp.dot(
            value.astype(jnp.bfloat16), in_order(out_ref, y, slice(0, NQ + NKV)), preferred_element_type=jnp.float32
        )
        total = part if total is None else total + part

    query = total[:, :NQ].astype(jnp.bfloat16)
    keyval = total[:, NQ:].astype(jnp.bfloat16)
    query_ref[...] = query
    keyval_ref[...] = keyval
    mine = place_ref[0]
    keep = positions(span_ref, mine, rows, 0) <= positions(span_ref, mine, rows, 1)
    key = keyval[:, :HEAD]
    value = keyval[:, HEAD:].T
    for h in range(QHEADS):
        cols = slice(h * HEAD, (h + 1) * HEAD)
        state = jnp.full((1, rows), -1e30, jnp.float32), jnp.zeros((1, rows), jnp.float32), None
        state = block_update(query[:, cols], key, value, keep, state)
        max_ref[h : h + 1, :] = state[0]
        sum_ref[h : h + 1, :] = state[1]
        wide_ref[:, cols] = state[2].T


def layer(place, spans, attended, gain, parts, weights):
    rows = attended.shape[0]
    depth = weights.shape[0]
    smem = pl.BlockSpec(memory_space=pltpu.SMEM)
    vmem = pl.BlockSpec(memory_space=pltpu.VMEM)
    anywhere = pl.BlockSpec(memory_space=pl.ANY)
    stat = jax.ShapeDtypeStruct((QHEADS, rows), jnp.float32)
    return pl.pallas_call(
        layer_kernel,
        out_shape=(
            jax.ShapeDtypeStruct((rows, NQ), jnp.bfloat16),
            jax.ShapeDtypeStruct((rows, NKV), jnp.bfloat16),
            stat,
            stat,
            jax.ShapeDtypeStruct((rows, NQ), jnp.float32),
        ),
        in_specs=[smem, smem, vmem, vmem] + [anywhere] * (len(parts) + 1),
        out_specs=(vmem,) * 5,
        scratch_shapes=[
            pltpu.VMEM((rows, depth), jnp.bfloat16),
            pltpu.VMEM(weights.shape, jnp.bfloat16),
            pltpu.SemaphoreType.DMA((len(STARTS),)),
            pltpu.SemaphoreType.DMA((NY,)),
        ],
        name="layer",
    )(place, spans, attended, gain, *parts, weights)


def per_device(
    resid,
    queries,
    keyvals,
    run_max,
    run_sum,
    run_out,
    span_pair,
    norm_gain,
    w_query,
    w_keyval,
    w_out,
):
    count = NY * NZ * NC
    my_index = lax.axis_index(CTX).astype(jnp.int32)
    my_x = lax.axis_index("x").astype(jnp.int32)
    spans = span_pair.T

    out_shard = lax.ppermute(w_out[0].T, SECT, ring(NS, 1))
    next_shard = jnp.concatenate([w_query[0], w_keyval[0]], axis=1)

    def along_z(shard):
        copies = jnp.broadcast_to(shard, (NZ, *shard.shape))
        return lax.all_to_all(copies, "zl", 0, 0, tiled=True).reshape(NZ * SHARD, -1)

    next_rows = along_z(next_shard)
    out_rows = along_z(out_shard)
    shards = jnp.concatenate([next_rows, out_rows], axis=1)
    weights = lax.all_gather(shards, ("y", "c"), axis=0, tiled=True)

    turn = [(s, (s + 1) % NX + s // NX * NX) for s in range(NS)]
    near = lax.ppermute(resid[0, STARTS[1] : STARTS[2]], SECT, turn)
    direct = lax.ppermute(resid[0, : STARTS[1]], SECT, ring(NS, 1))
    rest = resid[0, STARTS[2] :]
    back = [(s, s + 1) for s in range(0, NS, 2)] + [(s, s - 1) for s in range(NX - 1, NS, NX)]
    first = lax.ppermute(rest, SECT, [pair for pair in back if pair[0] % NX != NX - 3])
    near_block = lax.ppermute(keyvals[0], CTX, ring(count, -1))
    far_block = lax.ppermute(keyvals[0], CTX, ring(count, -2))
    attended = attend(
        my_index.reshape(1), spans, queries[0], far_block, near_block,
        run_max[0].T, run_sum[0].T, run_out[0],
    )
    attended_sent = lax.ppermute(attended, SECT, ring(NS, 1))
    far = lax.ppermute(near, SECT, [(0, NX), (NX, 0)])
    on = [(s, s + 1) for s in range(1, NS, NX)] + [(s, (s + 2) % NS) for s in range(2, NS, NX)]
    passing = jnp.where(my_x == 2, first, rest)
    second = lax.ppermute(passing, SECT, on)
    place = jnp.stack([my_index, (my_x > 0).astype(jnp.int32), my_x % 2])
    query_new, keyval_new, max_new, sum_new, out_new = layer(
        place, spans, attended_sent, norm_gain, (direct, near, far, first, second), weights
    )
    return (query_new[None], keyval_new[None], max_new.T[None], sum_new.T[None], out_new[None])


def solution(mesh):
    fine = Mesh(mesh.devices.reshape(2, NX, NY, NZ, NC), (*SECT, *CTX))
    rows = P(SECT, CTX, None)
    return jax.shard_map(
        per_device,
        mesh=fine,
        in_specs=(*[rows] * 6, P(), P(SECT, None), rows, rows, P(SECT, None, CTX)),
        out_specs=(rows,) * 5,
        check_vma=False,
    )
```

```python
import jax
import jax.numpy as jnp
from jax import lax
from jax.experimental import pallas as pl
from jax.experimental.pallas import tpu as pltpu
from jax.sharding import Mesh
from jax.sharding import PartitionSpec as P


HEAD = 128
QHEADS = 4
SECT = ("zh", "x")
CTX = ("y", "zl", "c")
NY, NZ, NC, NS = 8, 4, 2, 8
SHARD = 64
NX = 4
STARTS = (0, 80, 176)
BLOCK = NZ * NC * SHARD
NQ = QHEADS * HEAD
NKV = 2 * HEAD


def ring(count, steps):
    return [(source, (source + steps) % count) for source in range(count)]


def positions(span_ref, device, rows, axis):
    half = rows // 2
    shape = (rows, 1) if axis == 0 else (1, rows)
    offset = lax.broadcasted_iota(jnp.int32, shape, axis)
    first = span_ref[0, device] * half
    second = span_ref[1, device] * half - half
    return offset + jnp.where(offset < half, first, second)


def block_update(query, key, value, keep, old):
    scores = lax.dot_general(
        key, query, (((1,), (1,)), ((), ())), preferred_element_type=jnp.float32
    ) * HEAD ** (-0.5)
    masked = jnp.where(keep, scores, -1e30)
    old_max, old_sum, old_out = old
    new_max = jnp.maximum(old_max, jnp.max(masked, axis=0, keepdims=True))
    exp_scores = jnp.exp(masked - new_max)
    decay = jnp.exp(old_max - new_max)
    new_sum = old_sum * decay + jnp.sum(exp_scores, axis=0, keepdims=True)
    contrib = jnp.dot(value, exp_scores.astype(jnp.bfloat16), preferred_element_type=jnp.float32)
    new_out = contrib if old_out is None else old_out * decay + contrib
    return new_max, new_sum, new_out


def attend_kernel(index_ref, span_ref, query_ref, far_ref, near_ref, max_ref, sum_ref, out_ref, att_ref):
    count = NY * NZ * NC
    rows = query_ref.shape[0]
    mine = index_ref[0]
    pos_query = positions(span_ref, mine, rows, 1)
    blocks = []
    for hop, block_ref in ((2, far_ref), (1, near_ref)):
        keep = positions(span_ref, lax.rem(mine + hop, count), rows, 0) <= pos_query
        blocks.append((block_ref[:, :HEAD], block_ref[:, HEAD:].T, keep))
    for h in range(QHEADS):
        cols = slice(h * HEAD, (h + 1) * HEAD)
        state = max_ref[h : h + 1, :], sum_ref[h : h + 1, :], out_ref[:, cols].T
        for block in blocks:
            state = block_update(query_ref[:, cols], *block, state)
        att_ref[:, cols] = (state[2] / state[1]).T.astype(jnp.bfloat16)


def attend(my_index, spans, *operands):
    return pl.pallas_call(
        attend_kernel,
        out_shape=jax.ShapeDtypeStruct(operands[0].shape, jnp.bfloat16),
        in_specs=[pl.BlockSpec(memory_space=pltpu.SMEM)] * 2
        + [pl.BlockSpec(memory_space=pltpu.VMEM)] * len(operands),
        out_specs=pl.BlockSpec(memory_space=pltpu.VMEM),
        name="attend",
    )(my_index, spans, *operands)


def in_order(w_ref, y):
    parts = []
    for z in range(NZ):
        for c in range(NC):
            start = ((y * NC + c) * NZ + z) * SHARD
            parts.append(w_ref[start : start + SHARD, :])
    return jnp.concatenate(parts, axis=0)


def layer_kernel(
    place_ref,
    span_ref,
    att_ref,
    gain_ref,
    direct_ref,
    near_ref,
    far_ref,
    first_ref,
    second_ref,
    weight_ref,
    query_ref,
    keyval_ref,
    max_ref,
    sum_ref,
    wide_ref,
    resid_ref,
    out_ref,
    next_ref,
    row_sems,
    out_sems,
    next_sems,
):
    rows = query_ref.shape[0]

    def out_copy(y):
        block = pl.ds(y * BLOCK, BLOCK)
        source = weight_ref.at[block, pl.ds(NQ + NKV, NQ)]
        return pltpu.make_async_copy(source, out_ref.at[block, :], out_sems.at[y])

    def next_copy(y):
        block = pl.ds(y * BLOCK, BLOCK)
        source = weight_ref.at[block, pl.ds(0, NQ + NKV)]
        return pltpu.make_async_copy(source, next_ref.at[block, :], next_sems.at[y])

    def row_copy(source, part):
        block = resid_ref.at[pl.ds(STARTS[part], source.shape[0]), :]
        return pltpu.make_async_copy(source, block, row_sems.at[part])

    out_copy(0).start()
    row_copy(direct_ref, 0).start()

    for part, one, other in ((1, near_ref, far_ref), (2, first_ref, second_ref)):
        chosen = place_ref[part] > 0

        @pl.when(chosen)
        def _():
            row_copy(one, part).start()

        @pl.when(jnp.logical_not(chosen))
        def _():
            row_copy(other, part).start()

    for y in range(1, NY):
        out_copy(y).start()
    for part, source in enumerate((direct_ref, near_ref, first_ref)):
        row_copy(source, part).wait()

    total = None
    for y in range(NY):
        cols = slice(y * BLOCK, (y + 1) * BLOCK)
        out_copy(y).wait()
        next_copy(y).start()
        projected = lax.dot_general(
            att_ref[...],
            in_order(out_ref, y),
            (((1,), (1,)), ((), ())),
            preferred_element_type=jnp.float32,
        )
        finished = (resid_ref[:, cols].astype(jnp.float32) + projected).astype(jnp.bfloat16)
        square = finished.astype(jnp.float32)
        square = square * square
        part = sum(square[:, j * HEAD : (j + 1) * HEAD] for j in range(BLOCK // HEAD))
        total = part if total is None else total + part
        resid_ref[:, cols] = finished

    scale = lax.rsqrt(jnp.sum(total, axis=-1, keepdims=True) / (NY * BLOCK) + 1e-05)
    total = None
    for y in range(NY):
        cols = slice(y * BLOCK, (y + 1) * BLOCK)
        value = resid_ref[:, cols].astype(jnp.float32) * scale * gain_ref[:, cols]
        next_copy(y).wait()
        part = jnp.dot(
            value.astype(jnp.bfloat16), in_order(next_ref, y), preferred_element_type=jnp.float32
        )
        total = part if total is None else total + part

    query = total[:, :NQ].astype(jnp.bfloat16)
    keyval = total[:, NQ:].astype(jnp.bfloat16)
    query_ref[...] = query
    keyval_ref[...] = keyval
    mine = place_ref[0]
    keep = positions(span_ref, mine, rows, 0) <= positions(span_ref, mine, rows, 1)
    key = keyval[:, :HEAD]
    value = keyval[:, HEAD:].T
    for h in range(QHEADS):
        cols = slice(h * HEAD, (h + 1) * HEAD)
        state = jnp.full((1, rows), -1e30, jnp.float32), jnp.zeros((1, rows), jnp.float32), None
        state = block_update(query[:, cols], key, value, keep, state)
        max_ref[h : h + 1, :] = state[0]
        sum_ref[h : h + 1, :] = state[1]
        wide_ref[:, cols] = state[2].T


def layer(place, spans, attended, gain, parts, weights):
    rows = attended.shape[0]
    depth = weights.shape[0]
    smem = pl.BlockSpec(memory_space=pltpu.SMEM)
    vmem = pl.BlockSpec(memory_space=pltpu.VMEM)
    anywhere = pl.BlockSpec(memory_space=pl.ANY)
    stat = jax.ShapeDtypeStruct((QHEADS, rows), jnp.float32)
    return pl.pallas_call(
        layer_kernel,
        out_shape=(
            jax.ShapeDtypeStruct((rows, NQ), jnp.bfloat16),
            jax.ShapeDtypeStruct((rows, NKV), jnp.bfloat16),
            stat,
            stat,
            jax.ShapeDtypeStruct((rows, NQ), jnp.float32),
        ),
        in_specs=[smem, smem, vmem, vmem] + [anywhere] * (len(parts) + 1),
        out_specs=(vmem,) * 5,
        scratch_shapes=[
            pltpu.VMEM((rows, depth), jnp.bfloat16),
            pltpu.VMEM((depth, NQ), jnp.bfloat16),
            pltpu.VMEM((depth, NQ + NKV), jnp.bfloat16),
            pltpu.SemaphoreType.DMA((len(STARTS),)),
            pltpu.SemaphoreType.DMA((NY,)),
            pltpu.SemaphoreType.DMA((NY,)),
        ],
        name="layer",
    )(place, spans, attended, gain, *parts, weights)


def per_device(
    resid,
    queries,
    keyvals,
    run_max,
    run_sum,
    run_out,
    span_pair,
    norm_gain,
    w_query,
    w_keyval,
    w_out,
):
    count = NY * NZ * NC
    my_index = lax.axis_index(CTX).astype(jnp.int32)
    my_x = lax.axis_index("x").astype(jnp.int32)
    spans = span_pair.T

    out_shard = lax.ppermute(w_out[0].T, SECT, ring(NS, 1))
    next_shard = jnp.concatenate([w_query[0], w_keyval[0]], axis=1)

    def along_z(shard):
        copies = jnp.broadcast_to(shard, (NZ, *shard.shape))
        return lax.all_to_all(copies, "zl", 0, 0, tiled=True).reshape(NZ * SHARD, -1)

    next_rows = along_z(next_shard)
    out_rows = along_z(out_shard)
    shards = jnp.concatenate([next_rows, out_rows], axis=1)
    weights = lax.all_gather(shards, ("y", "c"), axis=0, tiled=True)

    turn = [(s, (s + 1) % NX + s // NX * NX) for s in range(NS)]
    near = lax.ppermute(resid[0, STARTS[1] : STARTS[2]], SECT, turn)
    direct = lax.ppermute(resid[0, : STARTS[1]], SECT, ring(NS, 1))
    rest = resid[0, STARTS[2] :]
    back = [(s, s + 1) for s in range(0, NS, 2)] + [(s, s - 1) for s in range(NX - 1, NS, NX)]
    first = lax.ppermute(rest, SECT, [pair for pair in back if pair[0] % NX != NX - 3])
    near_block = lax.ppermute(keyvals[0], CTX, ring(count, -1))
    far_block = lax.ppermute(keyvals[0], CTX, ring(count, -2))
    attended = attend(
        my_index.reshape(1), spans, queries[0], far_block, near_block,
        run_max[0].T, run_sum[0].T, run_out[0],
    )
    attended_sent = lax.ppermute(attended, SECT, ring(NS, 1))
    far = lax.ppermute(near, SECT, [(0, NX), (NX, 0)])
    on = [(s, s + 1) for s in range(1, NS, NX)] + [(s, (s + 2) % NS) for s in range(2, NS, NX)]
    passing = jnp.where(my_x == 2, first, rest)
    second = lax.ppermute(passing, SECT, on)
    place = jnp.stack([my_index, (my_x > 0).astype(jnp.int32), my_x % 2])
    query_new, keyval_new, max_new, sum_new, out_new = layer(
        place, spans, attended_sent, norm_gain, (direct, near, far, first, second), weights
    )
    return (query_new[None], keyval_new[None], max_new.T[None], sum_new.T[None], out_new[None])


def solution(mesh):
    fine = Mesh(mesh.devices.reshape(2, NX, NY, NZ, NC), (*SECT, *CTX))
    rows = P(SECT, CTX, None)
    return jax.shard_map(
        per_device,
        mesh=fine,
        in_specs=(*[rows] * 6, P(), P(SECT, None), rows, rows, P(SECT, None, CTX)),
        out_specs=(rows,) * 5,
        check_vma=False,
    )
```

```python
import jax
import jax.numpy as jnp
from jax import lax
from jax.experimental import pallas as pl
from jax.experimental.pallas import tpu as pltpu
from jax.sharding import Mesh
from jax.sharding import PartitionSpec as P


HEAD = 128
QHEADS = 4
SECT = ("zh", "x")
CTX = ("y", "zl", "c")
NY, NZ, NC, NS = 8, 4, 2, 8
SHARD = 64
NX = 4
STARTS = (0, 96, 176)
BLOCK = NZ * NC * SHARD
NQ = QHEADS * HEAD
NKV = 2 * HEAD


def ring(count, steps):
    return [(source, (source + steps) % count) for source in range(count)]


def positions(span_ref, device, rows, axis):
    half = rows // 2
    shape = (rows, 1) if axis == 0 else (1, rows)
    offset = lax.broadcasted_iota(jnp.int32, shape, axis)
    first = span_ref[0, device] * half
    second = span_ref[1, device] * half - half
    return offset + jnp.where(offset < half, first, second)


def block_update(query, key, value, keep, old):
    scores = lax.dot_general(
        key, query, (((1,), (1,)), ((), ())), preferred_element_type=jnp.float32
    ) * HEAD ** (-0.5)
    masked = jnp.where(keep, scores, -1e30)
    old_max, old_sum, old_out = old
    new_max = jnp.maximum(old_max, jnp.max(masked, axis=0, keepdims=True))
    exp_scores = jnp.exp(masked - new_max)
    decay = jnp.exp(old_max - new_max)
    new_sum = old_sum * decay + jnp.sum(exp_scores, axis=0, keepdims=True)
    contrib = jnp.dot(value, exp_scores.astype(jnp.bfloat16), preferred_element_type=jnp.float32)
    new_out = contrib if old_out is None else old_out * decay + contrib
    return new_max, new_sum, new_out


def attend_kernel(index_ref, span_ref, query_ref, far_ref, near_ref, max_ref, sum_ref, out_ref, att_ref):
    count = NY * NZ * NC
    rows = query_ref.shape[0]
    mine = index_ref[0]
    pos_query = positions(span_ref, mine, rows, 1)
    blocks = []
    for hop, block_ref in ((2, far_ref), (1, near_ref)):
        keep = positions(span_ref, lax.rem(mine + hop, count), rows, 0) <= pos_query
        blocks.append((block_ref[:, :HEAD], block_ref[:, HEAD:].T, keep))
    for h in range(QHEADS):
        cols = slice(h * HEAD, (h + 1) * HEAD)
        state = max_ref[h : h + 1, :], sum_ref[h : h + 1, :], out_ref[:, cols].T
        for block in blocks:
            state = block_update(query_ref[:, cols], *block, state)
        att_ref[:, cols] = (state[2] / state[1]).T.astype(jnp.bfloat16)


def attend(my_index, spans, *operands):
    return pl.pallas_call(
        attend_kernel,
        out_shape=jax.ShapeDtypeStruct(operands[0].shape, jnp.bfloat16),
        in_specs=[pl.BlockSpec(memory_space=pltpu.SMEM)] * 2
        + [pl.BlockSpec(memory_space=pltpu.VMEM)] * len(operands),
        out_specs=pl.BlockSpec(memory_space=pltpu.VMEM),
        name="attend",
    )(my_index, spans, *operands)


def in_order(w_ref, y, slots):
    parts = []
    for z in range(NZ):
        for c in range(NC):
            start = ((y * NC + c) * NZ + slots[z]) * SHARD
            if not isinstance(start, int):
                start = pl.multiple_of(start, SHARD)
            parts.append(w_ref[pl.ds(start, SHARD), :])
    return jnp.concatenate(parts, axis=0)


def layer_kernel(
    place_ref,
    span_ref,
    att_ref,
    gain_ref,
    direct_ref,
    near_ref,
    far_ref,
    first_ref,
    second_ref,
    weight_ref,
    query_ref,
    keyval_ref,
    max_ref,
    sum_ref,
    wide_ref,
    resid_ref,
    out_ref,
    next_ref,
    row_sems,
    out_sems,
    next_sems,
):
    rows = query_ref.shape[0]
    slots = [lax.rem(place_ref[3] - z + NZ, NZ) for z in range(NZ)]

    def out_copy(y):
        block = pl.ds(y * BLOCK, BLOCK)
        source = weight_ref.at[block, pl.ds(NQ + NKV, NQ)]
        return pltpu.make_async_copy(source, out_ref.at[block, :], out_sems.at[y])

    def next_copy(y):
        block = pl.ds(y * BLOCK, BLOCK)
        source = weight_ref.at[block, pl.ds(0, NQ + NKV)]
        return pltpu.make_async_copy(source, next_ref.at[block, :], next_sems.at[y])

    def row_copy(source, part):
        block = resid_ref.at[pl.ds(STARTS[part], source.shape[0]), :]
        return pltpu.make_async_copy(source, block, row_sems.at[part])

    out_copy(0).start()
    row_copy(direct_ref, 0).start()

    for part, one, other in ((1, near_ref, far_ref), (2, first_ref, second_ref)):
        chosen = place_ref[part] > 0

        @pl.when(chosen)
        def _():
            row_copy(one, part).start()

        @pl.when(jnp.logical_not(chosen))
        def _():
            row_copy(other, part).start()

    for y in range(1, NY):
        out_copy(y).start()
    for part, source in enumerate((direct_ref, near_ref, first_ref)):
        row_copy(source, part).wait()

    total = None
    for y in range(NY):
        cols = slice(y * BLOCK, (y + 1) * BLOCK)
        out_copy(y).wait()
        next_copy(y).start()
        projected = lax.dot_general(
            att_ref[...],
            in_order(out_ref, y, slots),
            (((1,), (1,)), ((), ())),
            preferred_element_type=jnp.float32,
        )
        finished = (resid_ref[:, cols].astype(jnp.float32) + projected).astype(jnp.bfloat16)
        square = finished.astype(jnp.float32)
        square = square * square
        part = sum(square[:, j * HEAD : (j + 1) * HEAD] for j in range(BLOCK // HEAD))
        total = part if total is None else total + part
        resid_ref[:, cols] = finished

    scale = lax.rsqrt(jnp.sum(total, axis=-1, keepdims=True) / (NY * BLOCK) + 1e-05)
    total = None
    for y in range(NY):
        cols = slice(y * BLOCK, (y + 1) * BLOCK)
        value = resid_ref[:, cols].astype(jnp.float32) * scale * gain_ref[:, cols]
        next_copy(y).wait()
        part = jnp.dot(
            value.astype(jnp.bfloat16), in_order(next_ref, y, range(NZ)), preferred_element_type=jnp.float32
        )
        total = part if total is None else total + part

    query = total[:, :NQ].astype(jnp.bfloat16)
    keyval = total[:, NQ:].astype(jnp.bfloat16)
    query_ref[...] = query
    keyval_ref[...] = keyval
    mine = place_ref[0]
    keep = positions(span_ref, mine, rows, 0) <= positions(span_ref, mine, rows, 1)
    key = keyval[:, :HEAD]
    value = keyval[:, HEAD:].T
    for h in range(QHEADS):
        cols = slice(h * HEAD, (h + 1) * HEAD)
        state = jnp.full((1, rows), -1e30, jnp.float32), jnp.zeros((1, rows), jnp.float32), None
        state = block_update(query[:, cols], key, value, keep, state)
        max_ref[h : h + 1, :] = state[0]
        sum_ref[h : h + 1, :] = state[1]
        wide_ref[:, cols] = state[2].T


def layer(place, spans, attended, gain, parts, weights):
    rows = attended.shape[0]
    depth = weights.shape[0]
    smem = pl.BlockSpec(memory_space=pltpu.SMEM)
    vmem = pl.BlockSpec(memory_space=pltpu.VMEM)
    anywhere = pl.BlockSpec(memory_space=pl.ANY)
    stat = jax.ShapeDtypeStruct((QHEADS, rows), jnp.float32)
    return pl.pallas_call(
        layer_kernel,
        out_shape=(
            jax.ShapeDtypeStruct((rows, NQ), jnp.bfloat16),
            jax.ShapeDtypeStruct((rows, NKV), jnp.bfloat16),
            stat,
            stat,
            jax.ShapeDtypeStruct((rows, NQ), jnp.float32),
        ),
        in_specs=[smem, smem, vmem, vmem] + [anywhere] * (len(parts) + 1),
        out_specs=(vmem,) * 5,
        scratch_shapes=[
            pltpu.VMEM((rows, depth), jnp.bfloat16),
            pltpu.VMEM((depth, NQ), jnp.bfloat16),
            pltpu.VMEM((depth, NQ + NKV), jnp.bfloat16),
            pltpu.SemaphoreType.DMA((len(STARTS),)),
            pltpu.SemaphoreType.DMA((NY,)),
            pltpu.SemaphoreType.DMA((NY,)),
        ],
        name="layer",
    )(place, spans, attended, gain, *parts, weights)


def per_device(
    resid,
    queries,
    keyvals,
    run_max,
    run_sum,
    run_out,
    span_pair,
    norm_gain,
    w_query,
    w_keyval,
    w_out,
):
    count = NY * NZ * NC
    my_index = lax.axis_index(CTX).astype(jnp.int32)
    my_x = lax.axis_index("x").astype(jnp.int32)
    my_z = lax.axis_index("zl").astype(jnp.int32)
    spans = span_pair.T

    out_parts = []
    for k in range(NZ):
        pairs = [
            (s * NZ + z, (s + 1) % NS * NZ + (z + k) % NZ) for s in range(NS) for z in range(NZ)
        ]
        out_parts.append(lax.ppermute(w_out[0].T, (*SECT, "zl"), pairs))
    next_shard = jnp.concatenate([w_query[0], w_keyval[0]], axis=1)
    next_copies = jnp.broadcast_to(next_shard, (NZ, SHARD, NQ + NKV))
    next_rows = lax.all_to_all(next_copies, "zl", 0, 0, tiled=True).reshape(NZ * SHARD, -1)
    shards = jnp.concatenate([next_rows, jnp.concatenate(out_parts)], axis=1)
    weights = lax.all_gather(shards, ("y", "c"), axis=0, tiled=True)

    turn = [(s, (s + 1) % NX + s // NX * NX) for s in range(NS)]
    near = lax.ppermute(resid[0, STARTS[1] : STARTS[2]], SECT, turn)
    direct = lax.ppermute(resid[0, : STARTS[1]], SECT, ring(NS, 1))
    rest = resid[0, STARTS[2] :]
    back = [(s, s + 1) for s in range(0, NS, 2)] + [(s, s - 1) for s in range(NX - 1, NS, NX)]
    first = lax.ppermute(rest, SECT, [pair for pair in back if pair[0] % NX != NX - 3])
    near_block = lax.ppermute(keyvals[0], CTX, ring(count, -1))
    far_block = lax.ppermute(keyvals[0], CTX, ring(count, -2))
    attended = attend(
        my_index.reshape(1), spans, queries[0], far_block, near_block,
        run_max[0].T, run_sum[0].T, run_out[0],
    )
    attended_sent = lax.ppermute(attended, SECT, ring(NS, 1))
    far = lax.ppermute(near, SECT, [(0, NX), (NX, 0)])
    on = [(s, s + 1) for s in range(1, NS, NX)] + [(s, (s + 2) % NS) for s in range(2, NS, NX)]
    passing = jnp.where(my_x == 2, first, rest)
    second = lax.ppermute(passing, SECT, on)
    place = jnp.stack([my_index, (my_x > 0).astype(jnp.int32), my_x % 2, my_z])
    query_new, keyval_new, max_new, sum_new, out_new = layer(
        place, spans, attended_sent, norm_gain, (direct, near, far, first, second), weights
    )
    return (query_new[None], keyval_new[None], max_new.T[None], sum_new.T[None], out_new[None])


def solution(mesh):
    fine = Mesh(mesh.devices.reshape(2, NX, NY, NZ, NC), (*SECT, *CTX))
    rows = P(SECT, CTX, None)
    return jax.shard_map(
        per_device,
        mesh=fine,
        in_specs=(*[rows] * 6, P(), P(SECT, None), rows, rows, P(SECT, None, CTX)),
        out_specs=(rows,) * 5,
        check_vma=False,
    )
```
